32 devices in a mesh: expert: 4 (over y, x), dp: 8 (over z, core).
Axes of the slice: x: 2, y: 2, z: 4, core: 2. Of those that a mesh axis runs over, the one named last changes fastest.
Arguments:
- gradient: bfloat16 [4, 8, 32, 4096], P('expert', 'dp'), may hold values from -6700 to 6700
- momentum: float32 [4, 32, 4096], P('expert'), may hold values from -4 to 4
- variance: bfloat16 [4, 32, 4096], P('expert'), may hold values from 0.0099487305 to 1
- worker_error: float32 [4, 8, 32, 4096], P('expert', 'dp'), may hold values from -6 to 6
- server_error: float32 [4, 32, 4096], P('expert', 'dp'), may hold values from -4 to 4
Outputs:
- new_momentum: float32 [4, 32, 4096], P('expert')
- adam_step: bfloat16 [4, 32, 4096], P('expert')
- new_worker_error: float32 [4, 8, 32, 4096], P('expert', 'dp')
- new_server_error: float32 [4, 32, 4096], P('expert', 'dp')
The draws below stay inside these ranges and needn't reach their ends.
All inputs are finite; a program needn't handle non-finite values. Where the reference program divides by a largest or mean magnitude, that divisor is 1e-20 or more.
Results may differ from the reference program's by a relative error of at most 0.011.
Values may be sent and summed in bfloat16 or wider, within the bound.
No kernel may reach another device: no remote copies, remote signals or barrier semaphores. Data moves between devices by JAX's collectives and lax.ppermute only.
A program may use at most 128 MiB of HBM per device.

```python
import math
import jax
import jax.numpy as jnp
from jax import lax

D = 4096
GROUP_ROWS = 4
EXPERTS = 4
REPLICAS = 8
ROWS = 32


def draw_gradient(key, part):
    base = jnp.clip(jax.random.normal(jax.random.fold_in(key, 11), (EXPERTS, REPLICAS, ROWS, D), jnp.float32), -6.0, 6.0)
    rising = 1.0 + (math.sqrt(3.0) - 1.0) * jnp.arange(EXPERTS, dtype=jnp.float32) / (EXPERTS - 1)
    pairing = jax.random.permutation(jax.random.fold_in(key, 12), REPLICAS)
    ranking = jax.random.permutation(jax.random.fold_in(key, 14), REPLICAS).astype(jnp.float32)
    levels = jnp.exp(-2.0 * math.log(10.0) * ranking / (REPLICAS - 1))
    owner_rows = jnp.arange(ROWS) // GROUP_ROWS
    paired = (owner_rows[None, :] == pairing[:, None]).astype(jnp.float32)
    spiked = 1.0 + 7.0 * paired
    values = 8.0 * base * rising[:, None, None, None] * levels[None, :, None, None] * spiked[None, :, :, None]
    return values.astype(jnp.bfloat16)


def with_spikes(entries, rng, source, target, blocks, factor):
    def block_of(position):
        return (jnp.arange(entries.shape[position]) // (entries.shape[position] // blocks)).reshape((-1,) + (1,) * (entries.ndim - 1 - position))

    near = jax.random.permutation(rng, blocks)[block_of(target)]
    other_side = (block_of(target) + blocks // 2) % blocks
    return jnp.where((block_of(source) == near) | (block_of(source) == other_side), factor * entries, entries)


def block_scale(key, shape, shards, least, high):
    def one(dim, blocks):
        steps = jax.random.uniform(jax.random.fold_in(jax.random.fold_in(key, 6), dim), (blocks,), jnp.float32, least / len(shards), high / len(shards))
        return jnp.repeat(jnp.exp(steps), shape[dim] // blocks).reshape((-1,) + (1,) * (len(shape) - dim - 1))

    level = one(*shards[0])
    for cut in shards[1:]:
        level = level * one(*cut)
    return level


def bell_draw(key, dims, scale, most, shards=(), kind=jnp.bfloat16):
    entries = jax.random.normal(key, dims, jnp.float32) * scale
    if len(shards) > 0:
        entries = block_scale(key, dims, shards, -0.22, 0.18) * entries
    return jnp.clip(entries, min=-most, max=most).astype(kind)


def bell_draw_with(rng, extent, spread, most, split, heavy, kind=jnp.bfloat16):
    array = spread * jax.random.normal(rng, extent, jnp.float32)
    if split:
        array = array * block_scale(rng, extent, split, -0.22, 0.18)
    return jnp.clip(with_spikes(array, jax.random.fold_in(rng, 3), *heavy), -most, most).astype(kind)


def setup_inputs(seed: int = 0) -> dict:
    streams_of = jax.random.split(jax.random.key(seed), 6)
    return {
        "gradient": draw_gradient(jax.random.fold_in(streams_of[5], 71), 0),
        "momentum": bell_draw(streams_of[1], (EXPERTS, ROWS, D), 0.25, 4.0, ((0, 4),), jnp.float32),
        "variance": jnp.clip(jnp.exp(math.log(1.0) - 4.61031033 * jax.random.uniform(streams_of[2], (EXPERTS, ROWS, D), jnp.float32) ** block_scale(streams_of[2], (EXPERTS, ROWS, D), ((0, 4),), -0.2, 0.2)), 0.0099487305, 1.0).astype(jnp.bfloat16),
        "worker_error": bell_draw_with(streams_of[3], (EXPERTS, REPLICAS, ROWS, D), 1.0, 6.0, ((0, 4), (1, 8)), (1, 2, 8, 2.0), jnp.float32),
        "server_error": bell_draw(streams_of[4], (EXPERTS, ROWS, D), 0.3, 4.0, ((0, 4), (1, 8)), jnp.float32),
    }


beta_one = 0.9
rms_limit = 5.0
scale_eps = 1e-06
adam_eps = 1e-08

def compress(values):
    row_scale = lax.optimization_barrier(jnp.mean(jnp.abs(values), axis=-1, keepdims=True)).astype(jnp.bfloat16)
    row_code = jnp.clip(values / (row_scale.astype(jnp.float32) + scale_eps), -1.0, 1.0).astype(jnp.bfloat16)
    decoded = row_scale.astype(jnp.float32) * row_code.astype(jnp.float32)
    return decoded

def reference(gradient, momentum, variance, worker_error, server_error):
    squares = lax.optimization_barrier(jnp.sum(jnp.square(gradient.astype(jnp.float32)), axis=(0, 2, 3)))
    root_mean = jnp.sqrt(squares / (EXPERTS * ROWS * D) + 1e-06)
    clip_factor = jnp.minimum(1.0, rms_limit / root_mean)

    def one_expert(items):
        grad_block, moment_block, variance_block, worker_block, server_block = items
        clipped = grad_block.astype(jnp.float32) * clip_factor[:, None, None]
        compensated = beta_one * moment_block[None] + (1.0 - beta_one) * clipped + worker_block
        decoded = compress(compensated)
        worker_new = compensated - decoded
        average = lax.optimization_barrier(jnp.sum(decoded, axis=0)) / REPLICAS
        combined = average + server_block
        owner_decoded = compress(combined)
        server_new = combined - owner_decoded
        step_out = (owner_decoded / (jnp.sqrt(variance_block.astype(jnp.float32)) + adam_eps)).astype(jnp.bfloat16)
        return (owner_decoded, step_out, worker_new, server_new)
    return lax.map(one_expert, (gradient, momentum, variance, worker_error, server_error))
```

```python
import jax
import jax.numpy as jnp
from jax import lax
from jax.sharding import PartitionSpec as P

beta_one = 0.9
rms_limit = 5.0
scale_eps = 1e-06
adam_eps = 1e-08


def stage_sizes(count):
    sizes = []
    for radix in (2, 4, 4, 4, 4):
        if count % radix == 0:
            sizes.append(radix)
            count //= radix
    for radix in range(2, count + 1):
        while count % radix == 0:
            sizes.append(radix)
            count //= radix
    return sizes


def partner(index, step, stride, radix):
    digit = (index // stride) % radix
    other = digit ^ step if radix & (radix - 1) == 0 else (digit + step) % radix
    return index + (other - digit) * stride


def swap(values, axis, step, stride, radix, count):
    pairs = [(i, partner(i, step, stride, radix)) for i in range(count)]
    return lax.ppermute(values, axis, pairs)


def peer_digit(digit, step, radix, back=False):
    if radix & (radix - 1) == 0:
        return digit ^ step
    return (digit + (radix - step if back else step)) % radix


def expert_sum(part):
    count = lax.axis_size("expert")
    total = part
    for step in range(1, count):
        total = total + swap(part, "expert", step, 1, count, count)
    return total


def compress(values):
    row_scale = jnp.mean(jnp.abs(values), axis=-1, keepdims=True).astype(jnp.bfloat16).astype(jnp.float32)
    row_code = jnp.clip(values / (row_scale + scale_eps), -1.0, 1.0).astype(jnp.bfloat16)
    return row_scale * row_code.astype(jnp.float32)


def scatter_sum(rows, replicas, group_rows):
    width = rows.shape[-1]
    place = lax.axis_index("dp")
    stride = 1
    held = rows.reshape(replicas, group_rows, width)
    for radix in stage_sizes(replicas):
        digit = (place // stride) % radix
        blocks = held.reshape(held.shape[0] // radix, radix, group_rows, width)
        total = lax.dynamic_index_in_dim(blocks, digit, 1, keepdims=False)
        for step in range(1, radix):
            piece = lax.dynamic_index_in_dim(blocks, peer_digit(digit, step, radix), 1, keepdims=False)
            got = swap(piece.astype(jnp.bfloat16), "dp", step, stride, radix, replicas)
            total = total + got.astype(jnp.float32)
        held = total
        stride *= radix
    return held[0]


def gather_rows(own, replicas):
    group_rows, width = own.shape
    place = lax.axis_index("dp")
    held = own[None]
    stride = replicas
    for radix in reversed(stage_sizes(replicas)):
        stride //= radix
        digit = (place // stride) % radix
        blocks = jnp.zeros((held.shape[0], radix) + own.shape, own.dtype)
        blocks = lax.dynamic_update_index_in_dim(blocks, held, digit, 1)
        for step in range(1, radix):
            got = swap(held, "dp", step, stride, radix, replicas)
            blocks = lax.dynamic_update_index_in_dim(blocks, got, peer_digit(digit, step, radix, True), 1)
        held = blocks.reshape(held.shape[0] * radix, group_rows, width)
    return held.reshape(replicas * group_rows, width)


def per_device(gradient, momentum, variance, worker_error, server_error):
    grad_local = gradient[0, 0].astype(jnp.float32)
    squares = expert_sum(jnp.sum(jnp.square(grad_local)).reshape(1, 1))
    entry_count = lax.axis_size("expert") * grad_local.shape[0] * grad_local.shape[1]
    root_mean = jnp.sqrt(squares / entry_count + 1e-06)
    clip_factor = jnp.minimum(1.0, rms_limit / root_mean)
    clipped = grad_local * clip_factor
    compensated = beta_one * momentum[0] + (1.0 - beta_one) * clipped + worker_error[0, 0]
    decoded = compress(compensated)
    worker_new = compensated - decoded
    replicas = lax.axis_size("dp")
    group_rows = server_error.shape[1]
    average = scatter_sum(decoded, replicas, group_rows) / replicas
    combined = average + server_error[0]
    owner_decoded = compress(combined)
    server_new = combined - owner_decoded
    momentum_new = gather_rows(owner_decoded.astype(jnp.bfloat16), replicas).astype(jnp.float32)
    step_out = (momentum_new / (jnp.sqrt(variance[0].astype(jnp.float32)) + adam_eps)).astype(
        jnp.bfloat16
    )
    return (momentum_new[None], step_out[None], worker_new[None, None], server_new[None])


def solution(mesh):
    placed = (
        P("expert", "dp", None, None),
        P("expert", None, None),
        P("expert", None, None),
        P("expert", "dp", None, None),
        P("expert", "dp", None),
    )
    return jax.shard_map(
        per_device,
        mesh=mesh,
        in_specs=placed,
        out_specs=(
            P("expert", None, None),
            P("expert", None, None),
            P("expert", "dp", None, None),
            P("expert", "dp", None),
        ),
        check_vma=False,
    )
```

```python
import functools
import math

import jax
import jax.numpy as jnp
from jax import lax
from jax.experimental import pallas as pl
from jax.experimental.pallas import tpu as pltpu
from jax.sharding import PartitionSpec as P


beta_one = 0.9
rms_limit = 5.0
scale_eps = 1e-06
adam_eps = 1e-08
CORES = 2
LANE_ROWS, LANES = 8, 128


def stage_sizes(count):
    sizes = []
    for radix in (2, 4, 4, 4, 4):
        if count % radix == 0:
            sizes.append(radix)
            count //= radix
    for radix in range(2, count + 1):
        while count % radix == 0:
            sizes.append(radix)
            count //= radix
    return sizes


def partner(index, step, stride, radix):
    digit = (index // stride) % radix
    other = digit ^ step if radix & (radix - 1) == 0 else (digit + step) % radix
    return index + (other - digit) * stride


def swap(values, axis, step, stride, radix, count):
    pairs = [(i, partner(i, step, stride, radix)) for i in range(count)]
    return lax.ppermute(values, axis, pairs)


def peer_digit(digit, step, radix, back=False):
    if radix & (radix - 1) == 0:
        return digit ^ step
    return (digit + (radix - step if back else step)) % radix


def expert_sum(part):
    count = lax.axis_size("expert")
    total = part
    for step in range(1, count):
        total = total + swap(part, "expert", step, 1, count, count)
    return total


def compress(values):
    row_scale = jnp.mean(jnp.abs(values), axis=-1, keepdims=True).astype(jnp.bfloat16).astype(jnp.float32)
    row_code = jnp.clip(values / (row_scale + scale_eps), -1.0, 1.0).astype(jnp.bfloat16)
    return row_scale * row_code.astype(jnp.float32)


def scatter_sum(rows, replicas, group_rows):
    width = rows.shape[-1]
    place = lax.axis_index("dp")
    stride = 1
    held = rows.reshape(replicas, group_rows, width)
    for radix in stage_sizes(replicas):
        digit = (place // stride) % radix
        blocks = held.reshape(held.shape[0] // radix, radix, group_rows, width)
        total = lax.dynamic_index_in_dim(blocks, digit, 1, keepdims=False)
        for step in range(1, radix):
            piece = lax.dynamic_index_in_dim(blocks, peer_digit(digit, step, radix), 1, keepdims=False)
            got = swap(piece.astype(jnp.bfloat16), "dp", step, stride, radix, replicas)
            total = total + got.astype(jnp.float32)
        held = total
        stride *= radix
    return held[0]


def gather_rows(own, replicas):
    group_rows, width = own.shape
    place = lax.axis_index("dp")
    held = own[None]
    stride = replicas
    for radix in reversed(stage_sizes(replicas)):
        stride //= radix
        digit = (place // stride) % radix
        blocks = jnp.zeros((held.shape[0], radix) + own.shape, own.dtype)
        blocks = lax.dynamic_update_index_in_dim(blocks, held, digit, 1)
        for step in range(1, radix):
            got = swap(held, "dp", step, stride, radix, replicas)
            blocks = lax.dynamic_update_index_in_dim(blocks, got, peer_digit(digit, step, radix, True), 1)
        held = blocks.reshape(held.shape[0] * radix, group_rows, width)
    return held.reshape(replicas * group_rows, width)


def per_device(gradient, momentum, variance, worker_error, server_error):
    grad_local = gradient[0, 0].astype(jnp.float32)
    squares = expert_sum(jnp.sum(jnp.square(grad_local)).reshape(1, 1))
    entry_count = lax.axis_size("expert") * grad_local.shape[0] * grad_local.shape[1]
    root_mean = jnp.sqrt(squares / entry_count + 1e-06)
    clip_factor = jnp.minimum(1.0, rms_limit / root_mean)
    clipped = grad_local * clip_factor
    compensated = beta_one * momentum[0] + (1.0 - beta_one) * clipped + worker_error[0, 0]
    decoded = compress(compensated)
    worker_new = compensated - decoded
    replicas = lax.axis_size("dp")
    group_rows = server_error.shape[1]
    average = scatter_sum(decoded, replicas, group_rows) / replicas
    combined = average + server_error[0]
    owner_decoded = compress(combined)
    server_new = combined - owner_decoded
    momentum_new = gather_rows(owner_decoded.astype(jnp.bfloat16), replicas).astype(jnp.float32)
    step_out = (momentum_new / (jnp.sqrt(variance[0].astype(jnp.float32)) + adam_eps)).astype(
        jnp.bfloat16
    )
    return (momentum_new[None], step_out[None], worker_new[None, None], server_new[None])


def kernel_call(body, outs, operands, scratch=(), out_space=None, in_space=None, vmem=16 << 20, flops=0):
    bytes_moved = sum(x.size * x.dtype.itemsize for x in operands) + sum(
        math.prod(shape) * jnp.dtype(kind).itemsize for shape, kind in outs
    )
    spaces = in_space or [pltpu.VMEM] * len(operands)
    out_spaces = out_space or [pltpu.VMEM] * len(outs)
    return pl.pallas_call(
        body,
        out_shape=[jax.ShapeDtypeStruct(shape, kind) for shape, kind in outs],
        in_specs=[pl.BlockSpec(memory_space=space) for space in spaces],
        out_specs=[pl.BlockSpec(memory_space=space) for space in out_spaces],
        scratch_shapes=list(scratch),
        compiler_params=pltpu.CompilerParams(vmem_limit_bytes=vmem),
        cost_estimate=pl.CostEstimate(flops=flops, bytes_accessed=bytes_moved, transcendentals=0),
    )(*operands)


def squares_kernel(grad_ref, out_ref):
    rows, width = grad_ref.shape
    total = [jnp.zeros((LANE_ROWS, LANES), jnp.float32) for _ in range(4)]
    turn = 0
    for row in range(0, rows, LANE_ROWS):
        for column in range(0, width, LANES):
            piece = grad_ref[row : row + LANE_ROWS, column : column + LANES].astype(jnp.float32)
            total[turn % 4] = total[turn % 4] + piece * piece
            turn += 1
    out_ref[...] = (total[0] + total[1]) + (total[2] + total[3])


def base_kernel(momentum_ref, error_ref, base_ref):
    for row in range(0, base_ref.shape[0], LANE_ROWS):
        rows = slice(row, row + LANE_ROWS)
        base_ref[rows, :] = beta_one * momentum_ref[rows, :] + error_ref[rows, :]


def row_scale_of(values):
    mean = jnp.sum(jnp.abs(values), axis=-1, keepdims=True) / values.shape[-1]
    return mean.astype(jnp.bfloat16).astype(jnp.float32)


def coded(values, scale):
    code = jnp.clip(values * (1.0 / (scale + scale_eps)), -1.0, 1.0).astype(jnp.bfloat16)
    return scale * code.astype(jnp.float32)


def worker_kernel(experts, chip_rows, chips, *refs):
    parts, (grad_ref, base_ref) = refs[:experts], refs[experts : experts + 2]
    outs = refs[experts + 2 : experts + 2 + chips]
    scale_ref, sum_ref = refs[experts + 2 + chips :]
    total = parts[0][...]
    for part in parts[1:]:
        total = total + part[...]
    count = experts * grad_ref.shape[0] * grad_ref.shape[1]
    squares = jnp.sum(total, axis=(0, 1), keepdims=True)
    factor = jnp.minimum(1.0, rms_limit / jnp.sqrt(squares / count + 1e-06))
    chip = lax.axis_index("dp") // CORES
    for step in reversed(range(chips)):
        rows = pl.ds(pl.multiple_of((chip ^ step) * chip_rows, chip_rows), chip_rows)
        values = base_ref[rows, :] + (1.0 - beta_one) * (grad_ref[rows, :].astype(jnp.float32) * factor)
        sum_ref[rows, :] = values
        scale = row_scale_of(values)
        scale_ref[rows, :] = jnp.broadcast_to(scale, (chip_rows, LANES))
        outs[step][...] = coded(values, scale).astype(outs[step].dtype)


def worker_error_kernel(chip_rows, scale_ref, sum_ref, variance_ref, new_hbm, root_ref, new_ref, sems):
    copies = []
    chunks = [slice(row, row + chip_rows) for row in range(0, sum_ref.shape[0], chip_rows)]
    for i, rows in enumerate(chunks):
        values = sum_ref[rows, :]
        new_ref[rows, :] = values - coded(values, scale_ref[rows, 0:1])
        copies.append(pltpu.make_async_copy(new_ref.at[rows, :], new_hbm.at[rows, :], sems.at[i]))
        copies[-1].start()
    for rows in chunks:
        root_ref[rows, :] = jnp.sqrt(variance_ref[rows, :].astype(jnp.float32)) + adam_eps
    for copy in copies:
        copy.wait()


def chip_sum_kernel(own_ref, *refs):
    total = own_ref[...]
    for got in refs[:-1]:
        total = total + got[...].astype(jnp.float32)
    refs[-1][...] = total.astype(jnp.bfloat16)


def combined_rows(replicas, own_ref, got_ref, error_ref):
    return (own_ref[...].astype(jnp.float32) + got_ref[...].astype(jnp.float32)) / replicas + error_ref[...]


def own_half(values):
    half = values.shape[0] // CORES
    first = lax.axis_index("dp") % CORES == 0
    return jnp.where(first, values[:half], values[half:])


def owner_kernel(replicas, own_ref, got_ref, error_ref, all_ref, half_ref):
    values = combined_rows(replicas, own_ref, got_ref, error_ref)
    decoded = coded(values, row_scale_of(values))
    all_ref[...] = decoded.astype(jnp.bfloat16)
    half_ref[...] = own_half(decoded).astype(jnp.bfloat16)


def server_error_kernel(replicas, own_ref, got_ref, error_ref, new_ref):
    values = combined_rows(replicas, own_ref, got_ref, error_ref)
    new_ref[...] = own_half(values - coded(values, row_scale_of(values)))


def final_kernel(chip_rows, own_ref, near_ref, far_ref, other_near_ref, other_far_ref, root_ref,
                 momentum_ref, step_ref, momentum_buf, step_buf, momentum_sem, step_sem):
    place = lax.axis_index("dp")
    chip, first = place // CORES, place % CORES == 0
    near = jnp.where(first, chip ^ 1, chip ^ 3)
    other_near = jnp.where(first, chip ^ 3, chip ^ 1)
    copies = []

    def put(slot, where, values):
        rows = pl.ds(pl.multiple_of(where * chip_rows, chip_rows), chip_rows)
        values = values.astype(jnp.float32)
        momentum_buf[slot] = values
        step_buf[slot] = (values / root_ref[rows, :]).astype(jnp.bfloat16)
        copies.append(pltpu.make_async_copy(momentum_buf.at[slot], momentum_ref.at[rows, :], momentum_sem.at[slot]))
        copies.append(pltpu.make_async_copy(step_buf.at[slot], step_ref.at[rows, :], step_sem.at[slot]))
        copies[-2].start()
        copies[-1].start()

    put(0, chip, own_ref[...])
    put(1, near, near_ref[...])
    put(2, other_near, other_near_ref[...])
    mine, other = far_ref[...].astype(jnp.float32), other_far_ref[...].astype(jnp.float32)
    put(3, chip ^ 2, jnp.where(first, jnp.concatenate([mine, other]), jnp.concatenate([other, mine])))
    for copy in copies:
        copy.wait()


def per_device_chips(gradient, momentum, variance, worker_error, server_error):
    experts, replicas = lax.axis_size("expert"), lax.axis_size("dp")
    chips = replicas // CORES
    rows, width = gradient.shape[2:]
    chip_rows = rows // chips
    half = server_error.shape[1]
    f32, bf16 = jnp.float32, jnp.bfloat16
    grad, moment, error = gradient[0, 0], momentum[0], worker_error[0, 0]

    (part,) = kernel_call(squares_kernel, [((LANE_ROWS, LANES), f32)], [grad], flops=2 * rows * width)
    parts = [part] + [swap(part, "expert", step, 1, experts, experts) for step in reversed(range(1, experts))]
    (base,) = kernel_call(base_kernel, [((rows, width), f32)], [moment, error], flops=2 * rows * width)
    other_error = swap(server_error[0], "dp", 1, 1, CORES, replicas)
    first = lax.axis_index("dp") % CORES == 0
    chip_error = jnp.where(
        first,
        jnp.concatenate([server_error[0], other_error]),
        jnp.concatenate([other_error, server_error[0]]),
    )

    outs = [((chip_rows, width), f32)] + [((chip_rows, width), bf16)] * (chips - 1)
    *sends, scales, sums = kernel_call(
        functools.partial(worker_kernel, experts, chip_rows, chips),
        outs + [((rows, LANES), f32), ((rows, width), f32)],
        parts + [grad, base],
        flops=20 * rows * width,
    )
    got = [swap(sends[step], "dp", step, CORES, chips, replicas) for step in reversed(range(1, chips))]
    worker_new, root = kernel_call(
        functools.partial(worker_error_kernel, chip_rows),
        [((rows, width), f32), ((rows, width), f32)],
        [scales, sums, variance[0]],
        out_space=[pltpu.HBM, pltpu.VMEM],
        scratch=[
            pltpu.VMEM((rows, width), f32),
            pltpu.SemaphoreType.DMA((chips,)),
        ],
        flops=20 * rows * width,
    )
    (chip_part,) = kernel_call(
        chip_sum_kernel, [((chip_rows, width), bf16)], [sends[0]] + got, flops=4 * chip_rows * width
    )
    other_part = swap(chip_part, "dp", 1, 1, CORES, replicas)
    decoded, decoded_half = kernel_call(
        functools.partial(owner_kernel, replicas),
        [((chip_rows, width), bf16), ((half, width), bf16)],
        [chip_part, other_part, chip_error],
        flops=20 * chip_rows * width,
    )
    near_pairs = [(i, i ^ (CORES if i % CORES == 0 else 3 * CORES)) for i in range(replicas)]
    near = lax.ppermute(decoded, "dp", near_pairs)
    far = swap(decoded_half, "dp", 2, CORES, chips, replicas)
    (server_new,) = kernel_call(
        functools.partial(server_error_kernel, replicas),
        [((half, width), f32)],
        [chip_part, other_part, chip_error],
        flops=20 * chip_rows * width,
    )
    other_near = swap(near, "dp", 1, 1, CORES, replicas)
    other_far = swap(far, "dp", 1, 1, CORES, replicas)
    momentum_new, step_out = kernel_call(
        functools.partial(final_kernel, chip_rows),
        [((rows, width), f32), ((rows, width), bf16)],
        [decoded, near, far, other_near, other_far, root],
        out_space=[pltpu.HBM, pltpu.HBM],
        scratch=[
            pltpu.VMEM((chips, chip_rows, width), f32),
            pltpu.VMEM((chips, chip_rows, width), bf16),
            pltpu.SemaphoreType.DMA((chips,)),
            pltpu.SemaphoreType.DMA((chips,)),
        ],
        flops=4 * rows * width,
    )
    return (momentum_new[None], step_out[None], worker_new[None, None], server_new[None])


def solution(mesh):
    if mesh.shape["dp"] == 4 * CORES:
        return placed_step(mesh, per_device_chips)
    return placed_step(mesh, per_device)


def placed_step(mesh, body):
    placed = (
        P("expert", "dp", None, None),
        P("expert", None, None),
        P("expert", None, None),
        P("expert", "dp", None, None),
        P("expert", "dp", None),
    )
    return jax.shard_map(
        body,
        mesh=mesh,
        in_specs=placed,
        out_specs=(
            P("expert", None, None),
            P("expert", None, None),
            P("expert", "dp", None, None),
            P("expert", "dp", None),
        ),
        check_vma=False,
    )
```

```python
import functools
import math

import jax
import jax.numpy as jnp
from jax import lax
from jax.experimental import pallas as pl
from jax.experimental.pallas import tpu as pltpu
from jax.sharding import PartitionSpec as P


beta_one = 0.9
rms_limit = 5.0
scale_eps = 1e-06
adam_eps = 1e-08
CORES = 2
LANE_ROWS, LANES = 8, 128
VMEM_LIMIT = 16 << 20


def stage_sizes(count):
    sizes = []
    for radix in (2, 4, 4, 4, 4):
        if count % radix == 0:
            sizes.append(radix)
            count //= radix
    for radix in range(2, count + 1):
        while count % radix == 0:
            sizes.append(radix)
            count //= radix
    return sizes


def partner(index, step, stride, radix):
    digit = (index // stride) % radix
    other = digit ^ step if radix & (radix - 1) == 0 else (digit + step) % radix
    return index + (other - digit) * stride


def swap(values, axis, step, stride, radix, count):
    pairs = [(i, partner(i, step, stride, radix)) for i in range(count)]
    return lax.ppermute(values, axis, pairs)


def peer_digit(digit, step, radix, back=False):
    if radix & (radix - 1) == 0:
        return digit ^ step
    return (digit + (radix - step if back else step)) % radix


def expert_sum(part):
    count = lax.axis_size("expert")
    total = part
    for step in range(1, count):
        total = total + swap(part, "expert", step, 1, count, count)
    return total


def compress(values):
    row_scale = jnp.mean(jnp.abs(values), axis=-1, keepdims=True).astype(jnp.bfloat16).astype(jnp.float32)
    row_code = jnp.clip(values / (row_scale + scale_eps), -1.0, 1.0).astype(jnp.bfloat16)
    return row_scale * row_code.astype(jnp.float32)


def scatter_sum(rows, replicas, group_rows):
    width = rows.shape[-1]
    place = lax.axis_index("dp")
    stride = 1
    held = rows.reshape(replicas, group_rows, width)
    for radix in stage_sizes(replicas):
        digit = (place // stride) % radix
        blocks = held.reshape(held.shape[0] // radix, radix, group_rows, width)
        total = lax.dynamic_index_in_dim(blocks, digit, 1, keepdims=False)
        for step in range(1, radix):
            piece = lax.dynamic_index_in_dim(blocks, peer_digit(digit, step, radix), 1, keepdims=False)
            got = swap(piece.astype(jnp.bfloat16), "dp", step, stride, radix, replicas)
            total = total + got.astype(jnp.float32)
        held = total
        stride *= radix
    return held[0]


def gather_rows(own, replicas):
    group_rows, width = own.shape
    place = lax.axis_index("dp")
    held = own[None]
    stride = replicas
    for radix in reversed(stage_sizes(replicas)):
        stride //= radix
        digit = (place // stride) % radix
        blocks = jnp.zeros((held.shape[0], radix) + own.shape, own.dtype)
        blocks = lax.dynamic_update_index_in_dim(blocks, held, digit, 1)
        for step in range(1, radix):
            got = swap(held, "dp", step, stride, radix, replicas)
            blocks = lax.dynamic_update_index_in_dim(blocks, got, peer_digit(digit, step, radix, True), 1)
        held = blocks.reshape(held.shape[0] * radix, group_rows, width)
    return held.reshape(replicas * group_rows, width)


def per_device(gradient, momentum, variance, worker_error, server_error):
    grad_local = gradient[0, 0].astype(jnp.float32)
    squares = expert_sum(jnp.sum(jnp.square(grad_local)).reshape(1, 1))
    entry_count = lax.axis_size("expert") * grad_local.shape[0] * grad_local.shape[1]
    root_mean = jnp.sqrt(squares / entry_count + 1e-06)
    clip_factor = jnp.minimum(1.0, rms_limit / root_mean)
    clipped = grad_local * clip_factor
    compensated = beta_one * momentum[0] + (1.0 - beta_one) * clipped + worker_error[0, 0]
    decoded = compress(compensated)
    worker_new = compensated - decoded
    replicas = lax.axis_size("dp")
    group_rows = server_error.shape[1]
    average = scatter_sum(decoded, replicas, group_rows) / replicas
    combined = average + server_error[0]
    owner_decoded = compress(combined)
    server_new = combined - owner_decoded
    momentum_new = gather_rows(owner_decoded.astype(jnp.bfloat16), replicas).astype(jnp.float32)
    step_out = (momentum_new / (jnp.sqrt(variance[0].astype(jnp.float32)) + adam_eps)).astype(
        jnp.bfloat16
    )
    return (momentum_new[None], step_out[None], worker_new[None, None], server_new[None])


def kernel_call(body, outs, operands, scratch=(), out_space=None, in_space=None, aliases=None, flops=0):
    bytes_moved = sum(x.size * x.dtype.itemsize for x in operands) + sum(
        math.prod(shape) * jnp.dtype(kind).itemsize for shape, kind in outs
    )
    spaces = in_space or [pltpu.VMEM] * len(operands)
    out_spaces = out_space or [pltpu.VMEM] * len(outs)
    return pl.pallas_call(
        body,
        out_shape=[jax.ShapeDtypeStruct(shape, kind) for shape, kind in outs],
        in_specs=[pl.BlockSpec(memory_space=space) for space in spaces],
        out_specs=[pl.BlockSpec(memory_space=space) for space in out_spaces],
        scratch_shapes=list(scratch),
        input_output_aliases=aliases or {},
        compiler_params=pltpu.CompilerParams(vmem_limit_bytes=VMEM_LIMIT),
        cost_estimate=pl.CostEstimate(flops=flops, bytes_accessed=bytes_moved, transcendentals=0),
    )(*operands)


def squares_kernel(grad_ref, out_ref):
    rows, width = grad_ref.shape
    total = [jnp.zeros((LANE_ROWS, LANES), jnp.float32) for _ in range(4)]
    turn = 0
    for row in range(0, rows, LANE_ROWS):
        for column in range(0, width, LANES):
            piece = grad_ref[row : row + LANE_ROWS, column : column + LANES].astype(jnp.float32)
            total[turn % 4] = total[turn % 4] + piece * piece
            turn += 1
    out_ref[...] = (total[0] + total[1]) + (total[2] + total[3])


def base_kernel(momentum_ref, error_ref, base_ref):
    for row in range(0, base_ref.shape[0], LANE_ROWS):
        rows = slice(row, row + LANE_ROWS)
        base_ref[rows, :] = beta_one * momentum_ref[rows, :] + error_ref[rows, :]


def row_scale_of(values):
    mean = jnp.sum(jnp.abs(values), axis=-1, keepdims=True) / values.shape[-1]
    return mean.astype(jnp.bfloat16).astype(jnp.float32)


def coded(values, scale):
    code = jnp.clip(values * (1.0 / (scale + scale_eps)), -1.0, 1.0).astype(jnp.bfloat16)
    return scale * code.astype(jnp.float32)


def position():
    place = lax.axis_index("dp")
    return place // CORES, place % CORES == 0


def chip_rows_at(chip, chip_rows):
    return pl.ds(pl.multiple_of(chip * chip_rows, chip_rows), chip_rows)


def pick_half(low, high, top):
    half = low.shape[0] // CORES
    return jnp.where(
        top, jnp.concatenate([low[:half], high[:half]]), jnp.concatenate([low[half:], high[half:]])
    )


def worker_kernel(experts, chip_rows, *refs):
    parts = refs[:experts]
    grad_ref, base_ref, same_ref, cross_ref, send_ref, scale_ref, sum_ref = refs[experts:]
    total = parts[0][...]
    for part in parts[1:]:
        total = total + part[...]
    count = experts * grad_ref.shape[0] * grad_ref.shape[1]
    squares = jnp.sum(total, axis=(0, 1), keepdims=True)
    factor = jnp.minimum(1.0, rms_limit / jnp.sqrt(squares / count + 1e-06))
    chip, first = position()
    for turn, mine_ref in enumerate((same_ref, cross_ref)):
        parity = (chip + turn) % 2
        decoded = []
        for block in (parity, parity + 2):
            rows = chip_rows_at(block, chip_rows)
            values = base_ref[rows, :] + (1.0 - beta_one) * (grad_ref[rows, :].astype(jnp.float32) * factor)
            sum_ref[rows, :] = values
            scale = row_scale_of(values)
            scale_ref[rows, :] = jnp.broadcast_to(scale, (chip_rows, LANES))
            decoded.append(coded(values, scale))
        mine_ref[...] = pick_half(*decoded, first)
        send_ref[turn * chip_rows : (turn + 1) * chip_rows, :] = pick_half(*decoded, jnp.logical_not(first)).astype(
            jnp.bfloat16
        )


def worker_error_kernel(chip_rows, scale_ref, sum_ref, variance_ref, new_hbm, inverse_ref, new_ref, sems):
    copies = []
    chunks = [slice(row, row + chip_rows) for row in range(0, sum_ref.shape[0], chip_rows)]
    for i, rows in enumerate(chunks):
        values = sum_ref[rows, :]
        new_ref[rows, :] = values - coded(values, scale_ref[rows, 0:1])
        copies.append(pltpu.make_async_copy(new_ref.at[rows, :], new_hbm.at[rows, :], sems.at[i]))
        copies[-1].start()
    for rows in chunks:
        inverse_ref[rows, :] = 1.0 / (jnp.sqrt(variance_ref[rows, :].astype(jnp.float32)) + adam_eps)
    for copy in copies:
        copy.wait()


def chip_sum_kernel(replicas, chip_rows, same_ref, cross_ref, got_ref, error_ref, same_out, cross_out):
    chip, _ = position()
    error = replicas * error_ref[...]
    none = jnp.zeros_like(error)
    owned = jnp.where(chip < 2, jnp.concatenate([error, none]), jnp.concatenate([none, error]))
    same_out[...] = (same_ref[...] + got_ref[:chip_rows, :].astype(jnp.float32) + owned).astype(jnp.bfloat16)
    cross_out[...] = (cross_ref[...] + got_ref[chip_rows:, :].astype(jnp.float32)).astype(jnp.bfloat16)


def owner_kernel(replicas, own_ref, near_ref, far_ref, across_ref, sum_ref, out_ref):
    own, near, far, across = (ref[...].astype(jnp.float32) for ref in (own_ref, near_ref, far_ref, across_ref))
    values = ((own + across) + (near + far)) / replicas
    sum_ref[...] = values
    out_ref[...] = coded(values, row_scale_of(values)).astype(jnp.bfloat16)


def server_error_kernel(sum_ref, new_ref):
    values = sum_ref[...]
    left = values - coded(values, row_scale_of(values))
    half = left.shape[0] // CORES
    chip, _ = position()
    new_ref[...] = jnp.where(chip < 2, left[:half], left[half:])


def result_kernel(chip_rows, turn, mine_ref, other_ref, inverse_ref, *refs):
    momentum_ref, step_ref, momentum_buf, step_buf, sems = refs[-5:]
    chip, first = position()
    parity = (chip + turn) % 2
    mine, other = mine_ref[...].astype(jnp.float32), other_ref[...].astype(jnp.float32)
    half = chip_rows // CORES
    copies = []
    for slot in range(2):
        part = slice(slot * half, (slot + 1) * half)
        values = jnp.where(
            first, jnp.concatenate([mine[part], other[part]]), jnp.concatenate([other[part], mine[part]])
        )
        rows = chip_rows_at(parity + 2 * slot, chip_rows)
        momentum_buf[slot] = values
        copies.append(pltpu.make_async_copy(momentum_buf.at[slot], momentum_ref.at[rows, :], sems.at[0, slot]))
        copies[-1].start()
        step_buf[slot] = (values * inverse_ref[rows, :]).astype(jnp.bfloat16)
        copies.append(pltpu.make_async_copy(step_buf.at[slot], step_ref.at[rows, :], sems.at[1, slot]))
        copies[-1].start()
    for copy in copies:
        copy.wait()


def result_rows(chip_rows, turn, mine, other, inverse, outs):
    rows, width = inverse.shape
    shapes = [((rows, width), jnp.float32), ((rows, width), jnp.bfloat16)]
    return kernel_call(
        functools.partial(result_kernel, chip_rows, turn),
        shapes,
        [mine, other, inverse, *outs],
        in_space=[pltpu.VMEM] * 3 + [pltpu.HBM] * len(outs),
        out_space=[pltpu.HBM] * 2,
        scratch=[
            pltpu.VMEM((2, chip_rows, width), jnp.float32),
            pltpu.VMEM((2, chip_rows, width), jnp.bfloat16),
            pltpu.SemaphoreType.DMA((2, 2)),
        ],
        aliases={3 + i: i for i in range(len(outs))},
        flops=2 * rows * width,
    )


def per_device_chips(gradient, momentum, variance, worker_error, server_error):
    experts, replicas = lax.axis_size("expert"), lax.axis_size("dp")
    chips = replicas // CORES
    rows, width = gradient.shape[2:]
    chip_rows = rows // chips
    half = server_error.shape[1]
    f32, bf16 = jnp.float32, jnp.bfloat16
    block = (chip_rows, width)
    grad, moment, error = gradient[0, 0], momentum[0], worker_error[0, 0]

    def chip_swap(values, step):
        return swap(values, "dp", step, CORES, chips, replicas)

    def core_swap(values):
        return swap(values, "dp", 1, 1, CORES, replicas)

    (part,) = kernel_call(squares_kernel, [((LANE_ROWS, LANES), f32)], [grad], flops=2 * rows * width)
    parts = [part] + [swap(part, "expert", step, 1, experts, experts) for step in reversed(range(1, experts))]
    (base,) = kernel_call(base_kernel, [((rows, width), f32)], [moment, error], flops=2 * rows * width)
    same, cross, send, scales, sums = kernel_call(
        functools.partial(worker_kernel, experts, chip_rows),
        [(block, f32), (block, f32), ((2 * chip_rows, width), bf16), ((rows, LANES), f32), ((rows, width), f32)],
        parts + [grad, base],
        flops=20 * rows * width,
    )
    got = core_swap(send)
    same_sum, cross_sum = kernel_call(
        functools.partial(chip_sum_kernel, replicas, chip_rows),
        [(block, bf16), (block, bf16)],
        [same, cross, got, server_error[0]],
        flops=4 * rows * width,
    )
    far = chip_swap(cross_sum, 3)
    across = chip_swap(same_sum, 2)
    near = chip_swap(cross_sum, 1)
    worker_new, inverse = kernel_call(
        functools.partial(worker_error_kernel, chip_rows),
        [((rows, width), f32), ((rows, width), f32)],
        [scales, sums, variance[0]],
        out_space=[pltpu.HBM, pltpu.VMEM],
        scratch=[pltpu.VMEM((rows, width), f32), pltpu.SemaphoreType.DMA((chips,))],
        flops=20 * rows * width,
    )
    combined, decoded = kernel_call(
        functools.partial(owner_kernel, replicas),
        [(block, f32), (block, bf16)],
        [same_sum, near, far, across],
        flops=20 * chip_rows * width,
    )
    cross_decoded = chip_swap(decoded, 1)
    cross_pairs = [(i, i ^ (CORES + 1)) for i in range(replicas)]
    other_cross = lax.ppermute(decoded, "dp", cross_pairs)
    other_decoded = core_swap(decoded)
    (server_new,) = kernel_call(server_error_kernel, [((half, width), f32)], [combined], flops=20 * chip_rows * width)
    outs = result_rows(chip_rows, 0, decoded, other_decoded, inverse, ())
    momentum_new, step_out = result_rows(chip_rows, 1, cross_decoded, other_cross, inverse, outs)
    return (momentum_new[None], step_out[None], worker_new[None, None], server_new[None])


def solution(mesh):
    if mesh.shape["dp"] == 4 * CORES:
        return placed_step(mesh, per_device_chips)
    return placed_step(mesh, per_device)


def placed_step(mesh, body):
    placed = (
        P("expert", "dp", None, None),
        P("expert", None, None),
        P("expert", None, None),
        P("expert", "dp", None, None),
        P("expert", "dp", None),
    )
    return jax.shard_map(
        body,
        mesh=mesh,
        in_specs=placed,
        out_specs=(
            P("expert", None, None),
            P("expert", None, None),
            P("expert", "dp", None, None),
            P("expert", "dp", None),
        ),
        check_vma=False,
    )
```

```python
import functools
import math

import jax
import jax.numpy as jnp
from jax import lax
from jax.experimental import pallas as pl
from jax.experimental.pallas import tpu as pltpu
from jax.sharding import PartitionSpec as P


beta_one = 0.9
rms_limit = 5.0
scale_eps = 1e-06
adam_eps = 1e-08
CORES = 2
LANE_ROWS, LANES = 8, 128
VMEM_LIMIT = 16 << 20


def stage_sizes(count):
    sizes = []
    for radix in (2, 4, 4, 4, 4):
        if count % radix == 0:
            sizes.append(radix)
            count //= radix
    for radix in range(2, count + 1):
        while count % radix == 0:
            sizes.append(radix)
            count //= radix
    return sizes


def partner(index, step, stride, radix):
    digit = (index // stride) % radix
    other = digit ^ step if radix & (radix - 1) == 0 else (digit + step) % radix
    return index + (other - digit) * stride


def swap(values, axis, step, stride, radix, count):
    pairs = [(i, partner(i, step, stride, radix)) for i in range(count)]
    return lax.ppermute(values, axis, pairs)


def peer_digit(digit, step, radix, back=False):
    if radix & (radix - 1) == 0:
        return digit ^ step
    return (digit + (radix - step if back else step)) % radix


def expert_sum(part):
    count = lax.axis_size("expert")
    total = part
    for step in range(1, count):
        total = total + swap(part, "expert", step, 1, count, count)
    return total


def compress(values):
    row_scale = jnp.mean(jnp.abs(values), axis=-1, keepdims=True).astype(jnp.bfloat16).astype(jnp.float32)
    row_code = jnp.clip(values / (row_scale + scale_eps), -1.0, 1.0).astype(jnp.bfloat16)
    return row_scale * row_code.astype(jnp.float32)


def scatter_sum(rows, replicas, group_rows):
    width = rows.shape[-1]
    place = lax.axis_index("dp")
    stride = 1
    held = rows.reshape(replicas, group_rows, width)
    for radix in stage_sizes(replicas):
        digit = (place // stride) % radix
        blocks = held.reshape(held.shape[0] // radix, radix, group_rows, width)
        total = lax.dynamic_index_in_dim(blocks, digit, 1, keepdims=False)
        for step in range(1, radix):
            piece = lax.dynamic_index_in_dim(blocks, peer_digit(digit, step, radix), 1, keepdims=False)
            got = swap(piece.astype(jnp.bfloat16), "dp", step, stride, radix, replicas)
            total = total + got.astype(jnp.float32)
        held = total
        stride *= radix
    return held[0]


def gather_rows(own, replicas):
    group_rows, width = own.shape
    place = lax.axis_index("dp")
    held = own[None]
    stride = replicas
    for radix in reversed(stage_sizes(replicas)):
        stride //= radix
        digit = (place // stride) % radix
        blocks = jnp.zeros((held.shape[0], radix) + own.shape, own.dtype)
        blocks = lax.dynamic_update_index_in_dim(blocks, held, digit, 1)
        for step in range(1, radix):
            got = swap(held, "dp", step, stride, radix, replicas)
            blocks = lax.dynamic_update_index_in_dim(blocks, got, peer_digit(digit, step, radix, True), 1)
        held = blocks.reshape(held.shape[0] * radix, group_rows, width)
    return held.reshape(replicas * group_rows, width)


def per_device(gradient, momentum, variance, worker_error, server_error):
    grad_local = gradient[0, 0].astype(jnp.float32)
    squares = expert_sum(jnp.sum(jnp.square(grad_local)).reshape(1, 1))
    entry_count = lax.axis_size("expert") * grad_local.shape[0] * grad_local.shape[1]
    root_mean = jnp.sqrt(squares / entry_count + 1e-06)
    clip_factor = jnp.minimum(1.0, rms_limit / root_mean)
    clipped = grad_local * clip_factor
    compensated = beta_one * momentum[0] + (1.0 - beta_one) * clipped + worker_error[0, 0]
    decoded = compress(compensated)
    worker_new = compensated - decoded
    replicas = lax.axis_size("dp")
    group_rows = server_error.shape[1]
    average = scatter_sum(decoded, replicas, group_rows) / replicas
    combined = average + server_error[0]
    owner_decoded = compress(combined)
    server_new = combined - owner_decoded
    momentum_new = gather_rows(owner_decoded.astype(jnp.bfloat16), replicas).astype(jnp.float32)
    step_out = (momentum_new / (jnp.sqrt(variance[0].astype(jnp.float32)) + adam_eps)).astype(
        jnp.bfloat16
    )
    return (momentum_new[None], step_out[None], worker_new[None, None], server_new[None])


def kernel_call(body, outs, operands, scratch=(), out_space=None, in_space=None, aliases=None, flops=0):
    bytes_moved = sum(x.size * x.dtype.itemsize for x in operands) + sum(
        math.prod(shape) * jnp.dtype(kind).itemsize for shape, kind in outs
    )
    spaces = in_space or [pltpu.VMEM] * len(operands)
    out_spaces = out_space or [pltpu.VMEM] * len(outs)
    return pl.pallas_call(
        body,
        out_shape=[jax.ShapeDtypeStruct(shape, kind) for shape, kind in outs],
        in_specs=[pl.BlockSpec(memory_space=space) for space in spaces],
        out_specs=[pl.BlockSpec(memory_space=space) for space in out_spaces],
        scratch_shapes=list(scratch),
        input_output_aliases=aliases or {},
        compiler_params=pltpu.CompilerParams(vmem_limit_bytes=VMEM_LIMIT),
        cost_estimate=pl.CostEstimate(flops=flops, bytes_accessed=bytes_moved, transcendentals=0),
    )(*operands)


def squares_of(grad_ref):
    rows, width = grad_ref.shape
    total = [jnp.zeros((LANE_ROWS, LANES), jnp.float32) for _ in range(4)]
    turn = 0
    for row in range(0, rows, LANE_ROWS):
        for column in range(0, width, LANES):
            piece = grad_ref[row : row + LANE_ROWS, column : column + LANES].astype(jnp.float32)
            total[turn % 4] = total[turn % 4] + piece * piece
            turn += 1
    return (total[0] + total[1]) + (total[2] + total[3])


def squares_kernel(grad_ref, out_ref):
    out_ref[...] = squares_of(grad_ref)


def both_squares_kernel(own_ref, other_grad_ref, out_ref):
    out_ref[:LANE_ROWS, :] = own_ref[...]
    out_ref[LANE_ROWS:, :] = squares_of(other_grad_ref)


def base_rows(momentum_ref, error_ref, rows):
    return beta_one * momentum_ref[rows, :] + error_ref[rows, :]


def prepare_kernel(chip_rows, momentum_ref, error_ref, other_error_ref, grad_ref, other_grad_ref, base_ref, *outs):
    chip, first = position()
    for turn in range(2):
        parity = (chip + turn) % 2
        block = slice(turn * chip_rows, (turn + 1) * chip_rows)
        low, high = (chip_rows_at(place, chip_rows) for place in (parity, parity + 2))
        for errors, grads, base_out, grad_out in ((error_ref, grad_ref, *outs[:2]), (other_error_ref, other_grad_ref, *outs[2:])):
            halves = [base_rows(momentum_ref, errors, rows) for rows in (low, high)]
            if errors is error_ref:
                base_ref[low, :], base_ref[high, :] = halves
            base_out[block, :] = pick_half(*halves, first)
            grad_out[block, :] = pick_half(*(grads[rows, :].astype(jnp.float32) for rows in (low, high)), first)


def row_scale_of(values):
    mean = jnp.sum(jnp.abs(values), axis=-1, keepdims=True) / values.shape[-1]
    return mean.astype(jnp.bfloat16).astype(jnp.float32)


def coded(values, scale):
    code = jnp.clip(values * (1.0 / (scale + scale_eps)), -1.0, 1.0).astype(jnp.bfloat16)
    return scale * code.astype(jnp.float32)


def position():
    place = lax.axis_index("dp")
    return place // CORES, place % CORES == 0


def chip_rows_at(chip, chip_rows):
    return pl.ds(pl.multiple_of(chip * chip_rows, chip_rows), chip_rows)


def pick_half(low, high, top):
    half = low.shape[0] // CORES
    return jnp.where(
        top, jnp.concatenate([low[:half], high[:half]]), jnp.concatenate([low[half:], high[half:]])
    )


def worker_kernel(replicas, experts, entries, chip_rows, *refs):
    parts = refs[:experts]
    base_ref, grad_ref, other_base_ref, other_grad_ref, error_ref, same_ref, cross_ref, gain_ref = refs[experts:]
    total = parts[0][...]
    for part in parts[1:]:
        total = total + part[...]
    gains = []
    for row in (0, LANE_ROWS):
        squares = jnp.sum(total[row : row + LANE_ROWS], axis=(0, 1), keepdims=True)
        factor = jnp.minimum(1.0, rms_limit / jnp.sqrt(squares / (experts * entries) + 1e-06))
        gains.append((1.0 - beta_one) * factor)
    gain_ref[...] = jnp.broadcast_to(gains[0], gain_ref.shape)
    chip, _ = position()
    error = replicas * error_ref[...]
    none = jnp.zeros_like(error)
    owned = jnp.where(chip < 2, jnp.concatenate([error, none]), jnp.concatenate([none, error]))
    for turn, out_ref in enumerate((same_ref, cross_ref)):
        block = slice(turn * chip_rows, (turn + 1) * chip_rows)
        values = base_ref[block, :] + gains[0] * grad_ref[block, :]
        other = other_base_ref[block, :] + gains[1] * other_grad_ref[block, :]
        total = coded(values, row_scale_of(values)) + coded(other, row_scale_of(other))
        if turn == 0:
            total = total + owned
        out_ref[...] = total.astype(jnp.bfloat16)


def worker_error_kernel(chip_rows, gain_ref, grad_ref, base_ref, variance_ref, new_hbm, inverse_ref, new_ref, sems):
    gain = gain_ref[0:1, 0:1]
    copies = []
    chunks = [slice(row, row + chip_rows) for row in range(0, base_ref.shape[0], chip_rows)]
    for i, rows in enumerate(chunks):
        values = base_ref[rows, :] + gain * grad_ref[rows, :].astype(jnp.float32)
        new_ref[rows, :] = values - coded(values, row_scale_of(values))
        copies.append(pltpu.make_async_copy(new_ref.at[rows, :], new_hbm.at[rows, :], sems.at[i]))
        copies[-1].start()
    for rows in chunks:
        inverse_ref[rows, :] = 1.0 / (jnp.sqrt(variance_ref[rows, :].astype(jnp.float32)) + adam_eps)
    for copy in copies:
        copy.wait()


def owner_kernel(replicas, own_ref, near_ref, far_ref, across_ref, sum_ref, out_ref):
    own, near, far, across = (ref[...].astype(jnp.float32) for ref in (own_ref, near_ref, far_ref, across_ref))
    values = ((own + across) + (near + far)) / replicas
    sum_ref[...] = values
    out_ref[...] = coded(values, row_scale_of(values)).astype(jnp.bfloat16)


def server_error_kernel(sum_ref, new_ref):
    values = sum_ref[...]
    left = values - coded(values, row_scale_of(values))
    half = left.shape[0] // CORES
    chip, _ = position()
    new_ref[...] = jnp.where(chip < 2, left[:half], left[half:])


def result_kernel(chip_rows, turn, mine_ref, other_ref, inverse_ref, *refs):
    momentum_ref, step_ref, momentum_buf, step_buf, sems = refs[-5:]
    chip, first = position()
    parity = (chip + turn) % 2
    mine, other = mine_ref[...].astype(jnp.float32), other_ref[...].astype(jnp.float32)
    half = chip_rows // CORES
    copies = []
    for slot in range(2):
        part = slice(slot * half, (slot + 1) * half)
        values = jnp.where(
            first, jnp.concatenate([mine[part], other[part]]), jnp.concatenate([other[part], mine[part]])
        )
        rows = chip_rows_at(parity + 2 * slot, chip_rows)
        momentum_buf[slot] = values
        copies.append(pltpu.make_async_copy(momentum_buf.at[slot], momentum_ref.at[rows, :], sems.at[0, slot]))
        copies[-1].start()
        step_buf[slot] = (values * inverse_ref[rows, :]).astype(jnp.bfloat16)
        copies.append(pltpu.make_async_copy(step_buf.at[slot], step_ref.at[rows, :], sems.at[1, slot]))
        copies[-1].start()
    for copy in copies:
        copy.wait()


def result_rows(chip_rows, turn, mine, other, inverse, outs):
    rows, width = inverse.shape
    shapes = [((rows, width), jnp.float32), ((rows, width), jnp.bfloat16)]
    return kernel_call(
        functools.partial(result_kernel, chip_rows, turn),
        shapes,
        [mine, other, inverse, *outs],
        in_space=[pltpu.VMEM] * 3 + [pltpu.HBM] * len(outs),
        out_space=[pltpu.HBM] * 2,
        scratch=[
            pltpu.VMEM((2, chip_rows, width), jnp.float32),
            pltpu.VMEM((2, chip_rows, width), jnp.bfloat16),
            pltpu.SemaphoreType.DMA((2, 2)),
        ],
        aliases={3 + i: i for i in range(len(outs))},
        flops=2 * rows * width,
    )


def per_device_chips(gradient, momentum, variance, worker_error, server_error):
    experts, replicas = lax.axis_size("expert"), lax.axis_size("dp")
    chips = replicas // CORES
    rows, width = gradient.shape[2:]
    chip_rows = rows // chips
    half = server_error.shape[1]
    f32, bf16 = jnp.float32, jnp.bfloat16
    block = (chip_rows, width)
    grad, moment, error = gradient[0, 0], momentum[0], worker_error[0, 0]

    def chip_swap(values, step):
        return swap(values, "dp", step, CORES, chips, replicas)

    def core_swap(values):
        return swap(values, "dp", 1, 1, CORES, replicas)

    other_grad = core_swap(grad)
    other_error = core_swap(error)
    (own_part,) = kernel_call(squares_kernel, [((LANE_ROWS, LANES), f32)], [grad], flops=10**9)
    (part,) = kernel_call(
        both_squares_kernel, [((CORES * LANE_ROWS, LANES), f32)], [own_part, other_grad], flops=2 * rows * width
    )
    parts = [part] + [swap(part, "expert", step, 1, experts, experts) for step in reversed(range(1, experts))]
    pair = (2 * chip_rows, width)
    base, *halves = kernel_call(
        functools.partial(prepare_kernel, chip_rows),
        [((rows, width), f32)] + [(pair, f32)] * 4,
        [moment, error, other_error, grad, other_grad],
        flops=4 * rows * width,
    )
    same_sum, cross_sum, gain = kernel_call(
        functools.partial(worker_kernel, replicas, experts, rows * width, chip_rows),
        [(block, bf16), (block, bf16), ((LANE_ROWS, LANES), f32)],
        [*parts, *halves, server_error[0]],
        flops=20 * rows * width,
    )
    far = chip_swap(cross_sum, 3)
    across = chip_swap(same_sum, 2)
    near = chip_swap(cross_sum, 1)
    worker_new, inverse = kernel_call(
        functools.partial(worker_error_kernel, chip_rows),
        [((rows, width), f32), ((rows, width), f32)],
        [gain, grad, base, variance[0]],
        out_space=[pltpu.HBM, pltpu.VMEM],
        scratch=[pltpu.VMEM((rows, width), f32), pltpu.SemaphoreType.DMA((chips,))],
        flops=20 * rows * width,
    )
    combined, decoded = kernel_call(
        functools.partial(owner_kernel, replicas),
        [(block, f32), (block, bf16)],
        [same_sum, near, far, across],
        flops=20 * chip_rows * width,
    )
    cross_decoded = chip_swap(decoded, 1)
    cross_pairs = [(i, i ^ (CORES + 1)) for i in range(replicas)]
    other_cross = lax.ppermute(decoded, "dp", cross_pairs)
    other_decoded = core_swap(decoded)
    (server_new,) = kernel_call(server_error_kernel, [((half, width), f32)], [combined], flops=20 * chip_rows * width)
    outs = result_rows(chip_rows, 0, decoded, other_decoded, inverse, ())
    momentum_new, step_out = result_rows(chip_rows, 1, cross_decoded, other_cross, inverse, outs)
    return (momentum_new[None], step_out[None], worker_new[None, None], server_new[None])


def solution(mesh):
    if mesh.shape["dp"] == 4 * CORES:
        return placed_step(mesh, per_device_chips)
    return placed_step(mesh, per_device)


def placed_step(mesh, body):
    placed = (
        P("expert", "dp", None, None),
        P("expert", None, None),
        P("expert", None, None),
        P("expert", "dp", None, None),
        P("expert", "dp", None),
    )
    return jax.shard_map(
        body,
        mesh=mesh,
        in_specs=placed,
        out_specs=(
            P("expert", None, None),
            P("expert", None, None),
            P("expert", "dp", None, None),
            P("expert", "dp", None),
        ),
        check_vma=False,
    )
```

```python
import functools
import math

import jax
import jax.numpy as jnp
from jax import lax
from jax.experimental import pallas as pl
from jax.experimental.pallas import tpu as pltpu
from jax.sharding import PartitionSpec as P


beta_one = 0.9
rms_limit = 5.0
scale_eps = 1e-06
adam_eps = 1e-08
CORES = 2
LANE_ROWS, LANES = 8, 128
VMEM_LIMIT = 16 << 20


def stage_sizes(count):
    sizes = []
    for radix in (2, 4, 4, 4, 4):
        if count % radix == 0:
            sizes.append(radix)
            count //= radix
    for radix in range(2, count + 1):
        while count % radix == 0:
            sizes.append(radix)
            count //= radix
    return sizes


def partner(index, step, stride, radix):
    digit = (index // stride) % radix
    other = digit ^ step if radix & (radix - 1) == 0 else (digit + step) % radix
    return index + (other - digit) * stride


def swap(values, axis, step, stride, radix, count):
    pairs = [(i, partner(i, step, stride, radix)) for i in range(count)]
    return lax.ppermute(values, axis, pairs)


def peer_digit(digit, step, radix, back=False):
    if radix & (radix - 1) == 0:
        return digit ^ step
    return (digit + (radix - step if back else step)) % radix


def expert_sum(part):
    count = lax.axis_size("expert")
    total = part
    for step in range(1, count):
        total = total + swap(part, "expert", step, 1, count, count)
    return total


def compress(values):
    row_scale = jnp.mean(jnp.abs(values), axis=-1, keepdims=True).astype(jnp.bfloat16).astype(jnp.float32)
    row_code = jnp.clip(values / (row_scale + scale_eps), -1.0, 1.0).astype(jnp.bfloat16)
    return row_scale * row_code.astype(jnp.float32)


def scatter_sum(rows, replicas, group_rows):
    width = rows.shape[-1]
    place = lax.axis_index("dp")
    stride = 1
    held = rows.reshape(replicas, group_rows, width)
    for radix in stage_sizes(replicas):
        digit = (place // stride) % radix
        blocks = held.reshape(held.shape[0] // radix, radix, group_rows, width)
        total = lax.dynamic_index_in_dim(blocks, digit, 1, keepdims=False)
        for step in range(1, radix):
            piece = lax.dynamic_index_in_dim(blocks, peer_digit(digit, step, radix), 1, keepdims=False)
            got = swap(piece.astype(jnp.bfloat16), "dp", step, stride, radix, replicas)
            total = total + got.astype(jnp.float32)
        held = total
        stride *= radix
    return held[0]


def gather_rows(own, replicas):
    group_rows, width = own.shape
    place = lax.axis_index("dp")
    held = own[None]
    stride = replicas
    for radix in reversed(stage_sizes(replicas)):
        stride //= radix
        digit = (place // stride) % radix
        blocks = jnp.zeros((held.shape[0], radix) + own.shape, own.dtype)
        blocks = lax.dynamic_update_index_in_dim(blocks, held, digit, 1)
        for step in range(1, radix):
            got = swap(held, "dp", step, stride, radix, replicas)
            blocks = lax.dynamic_update_index_in_dim(blocks, got, peer_digit(digit, step, radix, True), 1)
        held = blocks.reshape(held.shape[0] * radix, group_rows, width)
    return held.reshape(replicas * group_rows, width)


def per_device(gradient, momentum, variance, worker_error, server_error):
    grad_local = gradient[0, 0].astype(jnp.float32)
    squares = expert_sum(jnp.sum(jnp.square(grad_local)).reshape(1, 1))
    entry_count = lax.axis_size("expert") * grad_local.shape[0] * grad_local.shape[1]
    root_mean = jnp.sqrt(squares / entry_count + 1e-06)
    clip_factor = jnp.minimum(1.0, rms_limit / root_mean)
    clipped = grad_local * clip_factor
    compensated = beta_one * momentum[0] + (1.0 - beta_one) * clipped + worker_error[0, 0]
    decoded = compress(compensated)
    worker_new = compensated - decoded
    replicas = lax.axis_size("dp")
    group_rows = server_error.shape[1]
    average = scatter_sum(decoded, replicas, group_rows) / replicas
    combined = average + server_error[0]
    owner_decoded = compress(combined)
    server_new = combined - owner_decoded
    momentum_new = gather_rows(owner_decoded.astype(jnp.bfloat16), replicas).astype(jnp.float32)
    step_out = (momentum_new / (jnp.sqrt(variance[0].astype(jnp.float32)) + adam_eps)).astype(
        jnp.bfloat16
    )
    return (momentum_new[None], step_out[None], worker_new[None, None], server_new[None])


def kernel_call(body, outs, operands, scratch=(), out_space=None, in_space=None, aliases=None, flops=0):
    bytes_moved = sum(x.size * x.dtype.itemsize for x in operands) + sum(
        math.prod(shape) * jnp.dtype(kind).itemsize for shape, kind in outs
    )
    spaces = in_space or [pltpu.VMEM] * len(operands)
    out_spaces = out_space or [pltpu.VMEM] * len(outs)
    return pl.pallas_call(
        body,
        out_shape=[jax.ShapeDtypeStruct(shape, kind) for shape, kind in outs],
        in_specs=[pl.BlockSpec(memory_space=space) for space in spaces],
        out_specs=[pl.BlockSpec(memory_space=space) for space in out_spaces],
        scratch_shapes=list(scratch),
        input_output_aliases=aliases or {},
        compiler_params=pltpu.CompilerParams(vmem_limit_bytes=VMEM_LIMIT),
        cost_estimate=pl.CostEstimate(flops=flops, bytes_accessed=bytes_moved, transcendentals=0),
    )(*operands)


def squares_of(grad_ref):
    rows, width = grad_ref.shape
    total = [jnp.zeros((LANE_ROWS, LANES), jnp.float32) for _ in range(4)]
    turn = 0
    for row in range(0, rows, LANE_ROWS):
        for column in range(0, width, LANES):
            piece = grad_ref[row : row + LANE_ROWS, column : column + LANES].astype(jnp.float32)
            total[turn % 4] = total[turn % 4] + piece * piece
            turn += 1
    return (total[0] + total[1]) + (total[2] + total[3])


def squares_kernel(grad_ref, out_ref):
    out_ref[...] = squares_of(grad_ref)


def both_squares_kernel(own_ref, other_grad_ref, out_ref):
    out_ref[:LANE_ROWS, :] = own_ref[...]
    out_ref[LANE_ROWS:, :] = squares_of(other_grad_ref)


def base_rows(momentum_ref, error_ref, rows):
    return beta_one * momentum_ref[rows, :] + error_ref[rows, :]


def prepare_kernel(chip_rows, momentum_ref, error_ref, other_error_ref, grad_ref, other_grad_ref, base_ref, *outs):
    chip, first = position()
    for turn in range(2):
        parity = (chip + turn) % 2
        block = slice(turn * chip_rows, (turn + 1) * chip_rows)
        low, high = (chip_rows_at(place, chip_rows) for place in (parity, parity + 2))
        for errors, grads, base_out, grad_out in ((error_ref, grad_ref, *outs[:2]), (other_error_ref, other_grad_ref, *outs[2:])):
            halves = [base_rows(momentum_ref, errors, rows) for rows in (low, high)]
            if errors is error_ref:
                base_ref[low, :], base_ref[high, :] = halves
            base_out[block, :] = pick_half(*halves, first)
            grad_out[block, :] = pick_half(*(grads[rows, :].astype(jnp.float32) for rows in (low, high)), first)


def row_scale_of(values):
    mean = jnp.sum(jnp.abs(values), axis=-1, keepdims=True) / values.shape[-1]
    return mean.astype(jnp.bfloat16).astype(jnp.float32)


def coded(values, scale):
    code = jnp.clip(values * (1.0 / (scale + scale_eps)), -1.0, 1.0).astype(jnp.bfloat16)
    return scale * code.astype(jnp.float32)


def position():
    place = lax.axis_index("dp")
    return place // CORES, place % CORES == 0


def chip_rows_at(chip, chip_rows):
    return pl.ds(pl.multiple_of(chip * chip_rows, chip_rows), chip_rows)


def pick_half(low, high, top):
    half = low.shape[0] // CORES
    return jnp.where(
        top, jnp.concatenate([low[:half], high[:half]]), jnp.concatenate([low[half:], high[half:]])
    )


def worker_kernel(replicas, experts, entries, chip_rows, *refs):
    parts = refs[:experts]
    base_ref, grad_ref, other_base_ref, other_grad_ref, error_ref, same_ref, cross_ref, gain_ref = refs[experts:]
    own, near, heard, other_heard = (part[...] for part in parts)
    other_heard = jnp.concatenate([other_heard[LANE_ROWS:], other_heard[:LANE_ROWS]])
    total = (own + near) + (heard + other_heard)
    gains = []
    for row in (0, LANE_ROWS):
        squares = jnp.sum(total[row : row + LANE_ROWS], axis=(0, 1), keepdims=True)
        factor = jnp.minimum(1.0, rms_limit / jnp.sqrt(squares / (experts * entries) + 1e-06))
        gains.append((1.0 - beta_one) * factor)
    gain_ref[...] = jnp.broadcast_to(gains[0], gain_ref.shape)
    chip, _ = position()
    error = replicas * error_ref[...]
    none = jnp.zeros_like(error)
    owned = jnp.where(chip < 2, jnp.concatenate([error, none]), jnp.concatenate([none, error]))
    for turn, out_ref in enumerate((same_ref, cross_ref)):
        block = slice(turn * chip_rows, (turn + 1) * chip_rows)
        values = base_ref[block, :] + gains[0] * grad_ref[block, :]
        other = other_base_ref[block, :] + gains[1] * other_grad_ref[block, :]
        total = coded(values, row_scale_of(values)) + coded(other, row_scale_of(other))
        if turn == 0:
            total = total + owned
        out_ref[...] = total.astype(jnp.bfloat16)


def worker_error_kernel(chip_rows, gain_ref, grad_ref, base_ref, variance_ref, new_hbm, inverse_ref, new_ref, sems):
    gain = gain_ref[0:1, 0:1]
    copies = []
    chunks = [slice(row, row + chip_rows) for row in range(0, base_ref.shape[0], chip_rows)]
    for i, rows in enumerate(chunks):
        values = base_ref[rows, :] + gain * grad_ref[rows, :].astype(jnp.float32)
        new_ref[rows, :] = values - coded(values, row_scale_of(values))
        copies.append(pltpu.make_async_copy(new_ref.at[rows, :], new_hbm.at[rows, :], sems.at[i]))
        copies[-1].start()
    for rows in chunks:
        inverse_ref[rows, :] = 1.0 / (jnp.sqrt(variance_ref[rows, :].astype(jnp.float32)) + adam_eps)
    for copy in copies:
        copy.wait()


def owner_kernel(replicas, own_ref, near_ref, far_ref, across_ref, sum_ref, out_ref):
    own, near, far, across = (ref[...].astype(jnp.float32) for ref in (own_ref, near_ref, far_ref, across_ref))
    values = ((own + across) + (near + far)) / replicas
    sum_ref[...] = values
    out_ref[...] = coded(values, row_scale_of(values)).astype(jnp.bfloat16)


def server_error_kernel(sum_ref, new_ref):
    values = sum_ref[...]
    left = values - coded(values, row_scale_of(values))
    half = left.shape[0] // CORES
    chip, _ = position()
    new_ref[...] = jnp.where(chip < 2, left[:half], left[half:])


def result_kernel(chip_rows, turn, mine_ref, other_ref, inverse_ref, *refs):
    momentum_ref, step_ref, momentum_buf, step_buf, sems = refs[-5:]
    chip, first = position()
    parity = (chip + turn) % 2
    mine, other = mine_ref[...].astype(jnp.float32), other_ref[...].astype(jnp.float32)
    half = chip_rows // CORES
    copies = []
    for slot in range(2):
        part = slice(slot * half, (slot + 1) * half)
        values = jnp.where(
            first, jnp.concatenate([mine[part], other[part]]), jnp.concatenate([other[part], mine[part]])
        )
        rows = chip_rows_at(parity + 2 * slot, chip_rows)
        momentum_buf[slot] = values
        copies.append(pltpu.make_async_copy(momentum_buf.at[slot], momentum_ref.at[rows, :], sems.at[0, slot]))
        copies[-1].start()
        step_buf[slot] = (values * inverse_ref[rows, :]).astype(jnp.bfloat16)
        copies.append(pltpu.make_async_copy(step_buf.at[slot], step_ref.at[rows, :], sems.at[1, slot]))
        copies[-1].start()
    for copy in copies:
        copy.wait()


def result_rows(chip_rows, turn, mine, other, inverse, outs):
    rows, width = inverse.shape
    shapes = [((rows, width), jnp.float32), ((rows, width), jnp.bfloat16)]
    return kernel_call(
        functools.partial(result_kernel, chip_rows, turn),
        shapes,
        [mine, other, inverse, *outs],
        in_space=[pltpu.VMEM] * 3 + [pltpu.HBM] * len(outs),
        out_space=[pltpu.HBM] * 2,
        scratch=[
            pltpu.VMEM((2, chip_rows, width), jnp.float32),
            pltpu.VMEM((2, chip_rows, width), jnp.bfloat16),
            pltpu.SemaphoreType.DMA((2, 2)),
        ],
        aliases={3 + i: i for i in range(len(outs))},
        flops=2 * rows * width,
    )


def per_device_chips(gradient, momentum, variance, worker_error, server_error):
    experts, replicas = lax.axis_size("expert"), lax.axis_size("dp")
    chips = replicas // CORES
    rows, width = gradient.shape[2:]
    chip_rows = rows // chips
    half = server_error.shape[1]
    f32, bf16 = jnp.float32, jnp.bfloat16
    block = (chip_rows, width)
    grad, moment, error = gradient[0, 0], momentum[0], worker_error[0, 0]

    def chip_swap(values, step):
        return swap(values, "dp", step, CORES, chips, replicas)

    def core_swap(values):
        return swap(values, "dp", 1, 1, CORES, replicas)

    other_grad = core_swap(grad)
    other_error = core_swap(error)
    (own_part,) = kernel_call(squares_kernel, [((LANE_ROWS, LANES), f32)], [grad], flops=10**9)
    (part,) = kernel_call(
        both_squares_kernel, [((CORES * LANE_ROWS, LANES), f32)], [own_part, other_grad], flops=2 * rows * width
    )
    split_pairs = [
        (expert * replicas + place, (expert ^ (2 if place % CORES == 0 else 3)) * replicas + place)
        for expert in range(experts)
        for place in range(replicas)
    ]
    heard = lax.ppermute(part, ("expert", "dp"), split_pairs)
    near_part = swap(part, "expert", 1, 1, experts, experts)
    other_heard = core_swap(heard)
    parts = [part, near_part, heard, other_heard]
    pair = (2 * chip_rows, width)
    base, *halves = kernel_call(
        functools.partial(prepare_kernel, chip_rows),
        [((rows, width), f32)] + [(pair, f32)] * 4,
        [moment, error, other_error, grad, other_grad],
        flops=4 * rows * width,
    )
    same_sum, cross_sum, gain = kernel_call(
        functools.partial(worker_kernel, replicas, experts, rows * width, chip_rows),
        [(block, bf16), (block, bf16), ((LANE_ROWS, LANES), f32)],
        [*parts, *halves, server_error[0]],
        flops=20 * rows * width,
    )
    far = chip_swap(cross_sum, 3)
    across = chip_swap(same_sum, 2)
    near = chip_swap(cross_sum, 1)
    worker_new, inverse = kernel_call(
        functools.partial(worker_error_kernel, chip_rows),
        [((rows, width), f32), ((rows, width), f32)],
        [gain, grad, base, variance[0]],
        out_space=[pltpu.HBM, pltpu.VMEM],
        scratch=[pltpu.VMEM((rows, width), f32), pltpu.SemaphoreType.DMA((chips,))],
        flops=20 * rows * width,
    )
    combined, decoded = kernel_call(
        functools.partial(owner_kernel, replicas),
        [(block, f32), (block, bf16)],
        [same_sum, near, far, across],
        flops=20 * chip_rows * width,
    )
    cross_decoded = chip_swap(decoded, 1)
    cross_pairs = [(i, i ^ (CORES + 1)) for i in range(replicas)]
    other_cross = lax.ppermute(decoded, "dp", cross_pairs)
    other_decoded = core_swap(decoded)
    (server_new,) = kernel_call(server_error_kernel, [((half, width), f32)], [combined], flops=20 * chip_rows * width)
    outs = result_rows(chip_rows, 0, decoded, other_decoded, inverse, ())
    momentum_new, step_out = result_rows(chip_rows, 1, cross_decoded, other_cross, inverse, outs)
    return (momentum_new[None], step_out[None], worker_new[None, None], server_new[None])


def solution(mesh):
    if mesh.shape["dp"] == 4 * CORES and mesh.shape["expert"] == 4:
        return placed_step(mesh, per_device_chips)
    return placed_step(mesh, per_device)


def placed_step(mesh, body):
    placed = (
        P("expert", "dp", None, None),
        P("expert", None, None),
        P("expert", None, None),
        P("expert", "dp", None, None),
        P("expert", "dp", None),
    )
    return jax.shard_map(
        body,
        mesh=mesh,
        in_specs=placed,
        out_specs=(
            P("expert", None, None),
            P("expert", None, None),
            P("expert", "dp", None, None),
            P("expert", "dp", None),
        ),
        check_vma=False,
    )
```
